32 devices in a mesh: region: 2 (over x), ty: 16 (over z, y, core).
Axes of the slice: x: 2, y: 2, z: 4, core: 2. Of those that a mesh axis runs over, the one named last changes fastest.
Arguments:
- mask_init: float32 [32, 512, 512], P(('region', 'ty')), parts along dimension 0, may hold values from -1.6 to 1.6
- dual_init: float32 [32, 512, 512], P(('region', 'ty')), parts along dimension 0, may hold values from -1.5 to 1.5
- target: bfloat16 [32, 512, 512], P(('region', 'ty')), parts along dimension 0, may hold values from 0 to 1, as said below
- kernels: float32 [8, 2, 1024], replicated, may hold values from -9 to 9
- weights: float32 [8], replicated, may hold values from 0.1 to 1
Outputs:
- mask_final: float32 [32, 512, 512], P(('region', 'ty')), parts along dimension 0
- dual_final: float32 [32, 512, 512], P(('region', 'ty')), parts along dimension 0
The draws below stay inside these ranges and needn't reach their ends.
There are 2 independent parts, one for each index of `region`. The reference program is written for one: setup_inputs(seed, part) draws one part's arguments, and reference() takes and returns one part's arrays. A program takes and returns all parts, laid end to end along the dimension named above; an argument that names none is the same for every part. Nothing has to cross between parts.
Inputs may be any that keep to these rules, and one draw needn't show every extreme that they name: `target`: each entry is 0 or 1; wherever two tiles cover the same canvas position they hold the same value.
All inputs are finite; a program needn't handle non-finite values.
Results may differ from the reference program's by a relative error of at most 0.0045.
Values sent between devices are 32-bit elements; how exact they have to be, the bound alone decides.
A program may use at most 128 MiB of HBM per device.

```python
import math
import jax
import jax.numpy as jnp
from jax import lax

N = 512
INTERSECTION = 128
F = 32
KERNELS = 8
GRID_COLS = 4
ITERS = 2
TILES = 16


def smooth_field(coarse):
    spacing = 2 * N // F
    pixels = jnp.arange(N, dtype=jnp.int32)
    cell_index = pixels // spacing
    fraction = (pixels % spacing).astype(jnp.float32) / spacing
    top_rows = coarse[:, cell_index, :]
    low_rows = coarse[:, cell_index + 1, :]
    rowwise = top_rows * (1.0 - fraction)[None, :, None] + low_rows * fraction[None, :, None]
    west_cols = rowwise[:, :, cell_index]
    east_cols = rowwise[:, :, cell_index + 1]
    return west_cols * (1.0 - fraction)[None, None, :] + east_cols * fraction[None, None, :]


def draw_mask_init(key, part):
    spacing = 2 * N // F
    points = N // spacing + 1
    coarse_key, rough_key = jax.random.split(jax.random.fold_in(key, 11))
    coarse = jnp.clip(0.22 * jax.random.normal(coarse_key, (TILES, points, points), jnp.float32), -0.75, 0.75)
    rough = jax.random.uniform(rough_key, (TILES, N, N), jnp.float32, -0.8, 0.8)
    return smooth_field(coarse) + rough


def draw_kernels(key, part):
    kernel_key = jax.random.fold_in(key, 23)
    return jnp.clip(3.0 * jax.random.normal(kernel_key, (KERNELS, 2, F * F), jnp.float32), -9.0, 9.0)


def draw_target(key, part):
    stride = N - INTERSECTION
    grid_height = TILES // GRID_COLS * stride + INTERSECTION
    grid_width = GRID_COLS * stride + INTERSECTION
    block_side = N // 8
    blocks_high = (grid_height + block_side - 1) // block_side
    blocks_wide = (grid_width + block_side - 1) // block_side
    kind_key, phase_key, bits_key = jax.random.split(jax.random.fold_in(key, 37), 3)
    block_kinds = jax.random.randint(kind_key, (blocks_high, blocks_wide), 0, 4)
    block_phase = jax.random.randint(phase_key, (blocks_high, blocks_wide), 0, 2)
    random_bits = jax.random.randint(bits_key, (grid_height, grid_width), 0, 2)
    canvas_rows = jnp.arange(grid_height, dtype=jnp.int32)
    canvas_cols = jnp.arange(grid_width, dtype=jnp.int32)
    kind_pixels = block_kinds[canvas_rows // block_side][:, canvas_cols // block_side]
    phase_pixels = block_phase[canvas_rows // block_side][:, canvas_cols // block_side]
    vertical = (canvas_cols[None, :] + phase_pixels) % 2
    horizontal = (canvas_rows[:, None] + phase_pixels) % 2
    canvas = jnp.where(kind_pixels == 0, random_bits, jnp.where(kind_pixels == 3, horizontal, vertical))
    tile_ids = jnp.arange(TILES, dtype=jnp.int32)
    row_start = tile_ids // GRID_COLS * stride
    col_start = tile_ids % GRID_COLS * stride
    pixels = jnp.arange(N, dtype=jnp.int32)
    rows_index = row_start[:, None, None] + pixels[None, :, None]
    cols_index = col_start[:, None, None] + pixels[None, None, :]
    return canvas[rows_index, cols_index].astype(jnp.bfloat16)


def shard_levels(stream_key, extent, pieces, least, top_value):
    factor_of = 1.0
    for axis_at, shards_of in pieces:
        heights = jax.random.uniform(jax.random.fold_in(jax.random.fold_in(stream_key, 6), axis_at), (shards_of,), jnp.float32, least / len(pieces), top_value / len(pieces))
        factor_of = factor_of * jnp.repeat(jnp.exp(heights), extent[axis_at] // shards_of).reshape((-1,) + (1,) * (len(extent) - 1 - axis_at))
    return factor_of


def gaussian(rng, extent, deviation, limit, cuts=(), held_as=jnp.bfloat16):
    array = jax.random.normal(rng, extent, jnp.float32) * deviation
    if len(cuts) > 0:
        array = shard_levels(rng, extent, cuts, -0.22, 0.18) * array
    return jnp.clip(array, min=-limit, max=limit).astype(held_as)


def setup_inputs(seed: int = 0, part: int = 0) -> dict:
    splits = jax.random.split(jax.random.key(seed), 6)
    part_keys = jax.random.split(jax.random.fold_in(splits[5], part), 6)
    return {
        "mask_init": draw_mask_init(jax.random.fold_in(jax.random.fold_in(splits[5], part), 71), part),
        "dual_init": gaussian(part_keys[1], (TILES, N, N), 0.3, 1.5, ((0, 16),), jnp.float32),
        "target": draw_target(jax.random.fold_in(jax.random.fold_in(splits[5], part), 71), part),
        "kernels": draw_kernels(jax.random.fold_in(splits[5], 71), part),
        "weights": jnp.clip(jnp.exp(jax.random.uniform(splits[4], (KERNELS,), jnp.float32, math.log(0.1), math.log(1.0))), 0.1, 1.0),
    }


SHARPNESS = 8.0
THRESHOLD = 0.3
STEP_SIZE = 0.25
PENALTY = 1.0
PRECISE = lax.Precision.HIGHEST


def tables():
    pixels = jnp.arange(N, dtype=jnp.int32)
    frequencies = jnp.arange(F, dtype=jnp.int32) - F // 2
    phases = (frequencies[:, None] * pixels[None, :]) % N
    angles = phases.astype(jnp.float32) * (2.0 * math.pi / N)
    return jnp.cos(angles), -jnp.sin(angles)


def exact_dot(left_side, right_side, contract):
    return lax.dot_general(left_side, right_side, (contract, ((), ())), precision=PRECISE, preferred_element_type=jnp.float32)


def plain_dot(left_side, right_side, contract):
    return lax.dot_general(left_side, right_side, (contract, ((), ())), preferred_element_type=jnp.float32)


def kernel_field(kernel, spectrum_real, spectrum_imag, cos_table, sin_table, rows_low):
    kernel_real = kernel[0].reshape(F, F)
    kernel_imag = kernel[1].reshape(F, F)
    gated_real = kernel_real * spectrum_real - kernel_imag * spectrum_imag
    gated_imag = kernel_real * spectrum_imag + kernel_imag * spectrum_real
    band_real = exact_dot(gated_real, cos_table, ((1,), (0,))) + exact_dot(gated_imag, sin_table, ((1,), (0,)))
    band_imag = exact_dot(gated_imag, cos_table, ((1,), (0,))) - exact_dot(gated_real, sin_table, ((1,), (0,)))
    upper = jnp.concatenate([band_real, band_imag], axis=1)
    lower = jnp.concatenate([band_imag, -band_real], axis=1)
    stacked = jnp.concatenate([upper, lower], axis=0).astype(jnp.bfloat16)
    field = plain_dot(rows_low, stacked, ((0,), (0,))) / (N * N)
    return field[:, :N], field[:, N:]


def mask_gradient(mask, target, kernels, weights):
    cos_table, sin_table = tables()
    rows_exact = jnp.concatenate([cos_table, sin_table], axis=0)
    rows_low = rows_exact.astype(jnp.bfloat16)
    cos_low = cos_table.astype(jnp.bfloat16)
    sin_low = sin_table.astype(jnp.bfloat16)
    partial_band = plain_dot(rows_low, mask.astype(jnp.bfloat16), ((1,), (1,)))
    part_real = partial_band[:F]
    part_imag = partial_band[F:]
    spectrum_real = exact_dot(cos_table, part_real, ((1,), (1,))) - exact_dot(sin_table, part_imag, ((1,), (1,)))
    spectrum_imag = exact_dot(cos_table, part_imag, ((1,), (1,))) + exact_dot(sin_table, part_real, ((1,), (1,)))
    weight_total = jnp.sum(weights)

    def forward(summed, item):
        kernel, weight = item
        field_real, field_imag = kernel_field(kernel, spectrum_real, spectrum_imag, cos_table, sin_table, rows_low)
        return summed + weight * (field_real * field_real + field_imag * field_imag), None

    summed, unused = lax.scan(forward, jnp.zeros((N, N), jnp.float32), (kernels, weights))
    intensity = summed / weight_total
    resist = jax.nn.sigmoid(SHARPNESS * (intensity - THRESHOLD))
    slope = 2.0 * (resist - target.astype(jnp.float32)) * SHARPNESS * resist * (1.0 - resist)
    back_table = jnp.concatenate([jnp.concatenate([cos_low, -sin_low], axis=1), jnp.concatenate([sin_low, cos_low], axis=1)], axis=0)

    def backward(carry, item):
        adjoint_real, adjoint_imag = carry
        kernel, weight = item
        field_real, field_imag = kernel_field(kernel, spectrum_real, spectrum_imag, cos_table, sin_table, rows_low)
        weighted = jnp.concatenate([slope * field_real, slope * field_imag], axis=1).astype(jnp.bfloat16)
        turned = plain_dot(back_table, weighted, ((1,), (1,)))
        turned_real = turned[:F]
        turned_imag = turned[F:]
        back_real = exact_dot(cos_table, turned_real, ((1,), (1,))) - exact_dot(sin_table, turned_imag, ((1,), (1,)))
        back_imag = exact_dot(cos_table, turned_imag, ((1,), (1,))) + exact_dot(sin_table, turned_real, ((1,), (1,)))
        kernel_real = kernel[0].reshape(F, F)
        kernel_imag = kernel[1].reshape(F, F)
        portion = weight / weight_total
        new_real = adjoint_real + portion * (kernel_real * back_real + kernel_imag * back_imag)
        new_imag = adjoint_imag + portion * (kernel_real * back_imag - kernel_imag * back_real)
        return (new_real, new_imag), None

    zero_block = jnp.zeros((F, F), jnp.float32)
    adjoints, unused = lax.scan(backward, (zero_block, zero_block), (kernels, weights))
    adjoint_real, adjoint_imag = adjoints
    tail_real = exact_dot(adjoint_real, cos_table, ((1,), (0,))) + exact_dot(adjoint_imag, sin_table, ((1,), (0,)))
    tail_imag = exact_dot(adjoint_imag, cos_table, ((1,), (0,))) - exact_dot(adjoint_real, sin_table, ((1,), (0,)))
    tails = jnp.concatenate([tail_real, tail_imag], axis=0)
    return exact_dot(rows_exact, tails, ((0,), (0,))) * (2.0 / (N * N))


def consensus(shared):
    stride = N - INTERSECTION
    grid_height = (TILES // GRID_COLS) * stride + INTERSECTION
    grid_width = GRID_COLS * stride + INTERSECTION
    canvas = jnp.zeros((grid_height, grid_width), jnp.float32)
    coverage = jnp.zeros((grid_height, grid_width), jnp.float32)
    ones_block = jnp.ones((N, N), jnp.float32)

    def corner_of(tile_index):
        tile_index = tile_index.astype(jnp.int32)
        top_pixel = ((tile_index // GRID_COLS) * stride).astype(jnp.int32)
        left_pixel = ((tile_index % GRID_COLS) * stride).astype(jnp.int32)
        return tile_index, top_pixel, left_pixel

    def place(tile_index, carry):
        canvas, coverage = carry
        tile_index, top_pixel, left_pixel = corner_of(tile_index)
        piece = lax.dynamic_index_in_dim(shared, tile_index, 0, keepdims=False)
        block = lax.dynamic_slice(canvas, (top_pixel, left_pixel), (N, N)) + piece
        canvas = lax.dynamic_update_slice(canvas, block, (top_pixel, left_pixel))
        counted = lax.dynamic_slice(coverage, (top_pixel, left_pixel), (N, N)) + ones_block
        coverage = lax.dynamic_update_slice(coverage, counted, (top_pixel, left_pixel))
        return canvas, coverage

    canvas, coverage = lax.fori_loop(0, TILES, place, (canvas, coverage))

    def take(tile_index):
        tile_index, top_pixel, left_pixel = corner_of(tile_index)
        summed = lax.dynamic_slice(canvas, (top_pixel, left_pixel), (N, N))
        counted = lax.dynamic_slice(coverage, (top_pixel, left_pixel), (N, N))
        return summed / counted

    return lax.map(take, jnp.arange(TILES, dtype=jnp.int32))


def reference(mask_init, dual_init, target, kernels, weights):
    mask = mask_init
    dual = dual_init
    for iteration in range(ITERS):
        agreed = consensus(mask + dual)
        dual = dual + mask - agreed
        gradient = lax.map(lambda item: mask_gradient(item[0], item[1], kernels, weights), (mask, target))
        mask = mask - STEP_SIZE * (gradient + PENALTY * (mask - agreed + dual))
    return mask, dual
```

```python
import functools

import jax
import jax.numpy as jnp
import numpy as np
from jax import lax
from jax.experimental import pallas as pl
from jax.experimental.pallas import tpu as pltpu
from jax.sharding import PartitionSpec as P

GRID_COLS = 4
INTERSECTION = 128
SHARPNESS = 8.0
THRESHOLD = 0.3
STEP_SIZE = 0.25
PENALTY = 1.0
MESH = pl.DeviceIdType.MESH
BF16 = jnp.bfloat16


def split_host(table):
    table = table.astype(np.float32)
    high = table.astype(BF16)
    low = (table - high.astype(np.float32)).astype(BF16)
    return high, low


def host_tables(n, f):
    g = 2 * f
    freq = np.arange(f) - f // 2
    phase = 2.0 * np.pi * ((freq[:, None] * np.arange(n)[None, :]) % n) / n
    cos, sin = np.cos(phase), -np.sin(phase)
    rows = np.concatenate([cos, sin], 0)
    rows_hi, rows_lo = split_host(rows)
    row_side = np.concatenate([rows_hi, rows_lo], 0)
    col_wide = np.concatenate([np.tile(cos.T, (1, 4)), np.tile(sin.T, (1, 4))], 1)
    col_side = split_host(col_wide)[0]
    coarse = 2.0 * np.pi * ((np.arange(g)[:, None] * freq[None, :]) % g) / g
    er, ei = np.cos(coarse), np.sin(coarse)
    pair = np.eye(2)
    to_real = np.kron(pair, np.concatenate([er.T, -ei.T], 0))
    to_imag = np.kron(pair, np.concatenate([ei.T, er.T], 0))
    lane_turn = np.concatenate([to_real, to_imag], 1)
    lane_fwd = np.concatenate(split_host(lane_turn / (n * n)), 1)
    lane_back = np.concatenate(split_host(lane_turn.T), 1)
    row_turn = np.concatenate([np.concatenate([er, -ei], 1), np.concatenate([ei, er], 1)], 0)
    turn_hi, turn_lo = split_host(row_turn)
    row_fwd = np.concatenate([turn_hi, turn_lo, turn_hi, turn_lo], 1)
    row_back = np.concatenate(split_host(row_turn.T), 0)
    half = np.arange(-(f - 1), f)
    angle = np.arange(n)[:, None] * f * 2 - np.arange(g)[None, :] * n
    spread = np.cos(2.0 * np.pi * ((angle[..., None] * half) % (n * g)) / (n * g)).sum(-1) / g
    s_hi, s_lo = split_host(spread)
    up_cols = np.concatenate([s_hi.T, s_lo.T, s_hi.T, s_lo.T], 0)
    er_low, ei_low = rows_hi[:f].T, -rows_hi[f:].T
    low_turn = np.concatenate([np.concatenate([er_low, -ei_low], 1), np.concatenate([ei_low, er_low], 1)], 0)
    up_rows = np.concatenate([low_turn, low_turn], 1)
    down_cols = np.concatenate([s_hi, s_hi, s_lo, s_lo], 1)
    scale = 2.0 / (n * n)
    c_hi, c_lo = split_host(cos * scale)
    t_hi, t_lo = split_host(sin * scale)
    tail_r = np.concatenate([c_hi, c_lo, t_hi, t_lo], 0)
    tail_i = np.concatenate([-t_hi, -t_lo, c_hi, c_lo], 0)
    tail = np.concatenate([tail_r, tail_i], 1)
    tail_tab = np.concatenate([tail, tail], 0)
    grad_rows = np.concatenate([rows_hi.T, rows_lo.T, rows_hi.T, rows_lo.T], 1)
    return [
        np.asarray(t, dtype=BF16)
        for t in (row_side, col_side, lane_fwd, row_fwd, up_cols, up_rows, down_cols, row_back, lane_back, tail_tab, grad_rows)
    ]


def dot(a, b):
    return lax.dot_general(a, b, (((1,), (0,)), ((), ())), preferred_element_type=jnp.float32)


def split(x):
    high = x.astype(BF16)
    return high, (x - high.astype(jnp.float32)).astype(BF16)


def stacked(x):
    high, low = split(x)
    return jnp.concatenate([high, high, low, low], axis=0)


def body(
    n, f, edge, count,
    mask_ref, dual_ref, target_ref, h_ref, w_ref,
    row_side, col_side, lane_fwd, row_fwd, up_cols, up_rows, down_cols, row_back, lane_back, tail_tab, grad_rows,
    mask_out, dual_out,
    shared, ring_s, ring_m, from_h_s, from_h_m, from_v_s, from_v_m, agreed, slope, adj, adj_in,
    send_sem, recv_sem,
):
    far = n - edge
    g = 2 * f
    me = lax.axis_index("ty")
    row, col = me // GRID_COLS, me % GRID_COLS
    grid_rows = count // GRID_COLS
    left, right = col > 0, col < GRID_COLS - 1
    upper, lower = row > 0, row < grid_rows - 1
    near = [
        (-1, left), (1, right), (-GRID_COLS, upper), (GRID_COLS, lower),
        (-GRID_COLS - 1, jnp.logical_and(upper, left)), (-GRID_COLS + 1, jnp.logical_and(upper, right)),
        (GRID_COLS - 1, jnp.logical_and(lower, left)), (GRID_COLS + 1, jnp.logical_and(lower, right)),
    ]
    opposite = [1, 0, 3, 2, 7, 6, 5, 4]

    barrier = pltpu.get_barrier_semaphore()
    for shift, there in near:
        @pl.when(there)
        def _(shift=shift):
            pl.semaphore_signal(barrier, inc=1, device_id={"ty": me + shift}, device_id_type=MESH)

    counter = [0]

    def remote(src, dst, to):
        index = counter[0]
        counter[0] += 1
        copy = pltpu.make_async_remote_copy(
            src_ref=src, dst_ref=dst, send_sem=send_sem.at[index], recv_sem=recv_sem.at[index],
            device_id={"ty": me + near[to][0]}, device_id_type=MESH,
        )
        return copy, near[to][1], near[opposite[to]][1]

    def start(entry):
        pl.when(entry[1])(entry[0].start)

    def arrived(entry):
        pl.when(entry[2])(entry[0].wait_recv)

    def sent(entry):
        pl.when(entry[1])(entry[0].wait_send)

    bands = (pl.ds(0, edge), pl.ds(far, edge))
    middle = pl.ds(edge, far - edge)

    def side_copies(src, dst, rows):
        return [
            remote(src.at[rows, bands[0]], dst.at[1, rows, :], 0),
            remote(src.at[rows, bands[1]], dst.at[0, rows, :], 1),
        ]

    src_mask = mask_ref.at[0]
    plan = {}
    for name, src, from_h, from_v, ring in (
        ("s", shared, from_h_s, from_v_s, ring_s),
        ("m", src_mask, from_h_m, from_v_m, ring_m),
    ):
        plan[name, "h"] = side_copies(src, from_h, bands[0]) + side_copies(src, from_h, bands[1])
        plan[name, "hm"] = side_copies(src, from_h, middle)
        plan[name, "v"] = [
            remote(src.at[bands[0], middle], from_v.at[1, :, middle], 2),
            remote(src.at[bands[1], middle], from_v.at[0, :, middle], 3),
        ]
        plan[name, "vc"] = [
            remote(ring.at[v, h], from_v.at[1 - v, :, bands[h]], 2 + v) for v in range(2) for h in range(2)
        ]
    plan["adj"] = [remote(adj, adj_in.at[opposite[to]], to) for to in range(8)]

    for h in range(2):
        @pl.when(jnp.logical_not(near[h][1]))
        def _(h=h):
            from_h_s[h] = jnp.zeros((n, edge), jnp.float32)
            from_h_m[h] = jnp.zeros((n, edge), jnp.float32)

        @pl.when(jnp.logical_not(near[2 + h][1]))
        def _(h=h):
            from_v_s[h] = jnp.zeros((edge, n), jnp.float32)
            from_v_m[h] = jnp.zeros((edge, n), jnp.float32)
    for to in range(8):
        @pl.when(jnp.logical_not(near[to][1]))
        def _(to=to):
            adj_in[to] = jnp.zeros((f, 4 * f), jnp.float32)

    shared[...] = mask_ref[0] + dual_ref[0]
    expected = sum(there.astype(jnp.int32) for _, there in near)
    pl.semaphore_wait(barrier, expected)

    for entry in plan["s", "h"] + plan["s", "v"] + plan["s", "hm"]:
        start(entry)

    quarters = w_ref.shape[0] // 2
    lane = lax.broadcasted_iota(jnp.int32, (1, 4 * f), 1)
    total = w_ref[0]
    for k in range(1, w_ref.shape[0]):
        total = total + w_ref[k]
    portions = [
        jnp.where(lane < 2 * f, w_ref[2 * k], w_ref[2 * k + 1]) / jnp.full((1, 4 * f), total, jnp.float32)
        for k in range(quarters)
    ]
    h_one = h_ref[...]
    is_real = (lane // f) % 2 == 0
    h_two = jnp.where(is_real, -pltpu.roll(h_one, 3 * f, 1), pltpu.roll(h_one, f, 1))

    def fields(mask_low):
        part = dot(row_side[...], mask_low)
        part = part[: 2 * f] + part[2 * f :]
        grid = dot(jnp.concatenate(split(part), axis=0), col_side[...])
        w = 8 * f
        grid = grid[: 2 * f] + grid[2 * f :]
        real = grid[:f, : 4 * f] - grid[f:, 4 * f :]
        imag = grid[:f, 4 * f :] + grid[f:, : 4 * f]
        real = jnp.concatenate([real] * quarters, axis=0)
        imag = jnp.concatenate([imag] * quarters, axis=0)
        gated = h_one * real + h_two * imag
        turned = dot(jnp.concatenate(split(gated), axis=0), lane_fwd[...])
        m = quarters * f
        turned = (turned[:m, :w] + turned[:m, w:]) + turned[m:, :w]
        wide = jnp.concatenate(
            [
                jnp.concatenate([turned[k * f : (k + 1) * f, : 4 * f], turned[k * f : (k + 1) * f, 4 * f :]], axis=0)
                for k in range(quarters)
            ],
            axis=1,
        )
        return dot(row_fwd[...], stacked(wide)), jnp.concatenate(split(wide), axis=0)

    def write_slope(waves):
        for r in range(0, n, edge):
            real = dot(up_rows[r : r + edge, :], waves)
            imag = dot(up_rows[n + r : n + r + edge, :], waves)
            energy = real * real + imag * imag
            summed = energy[:, : 2 * g] * portions[0]
            for k in range(1, quarters):
                summed = summed + energy[:, 2 * g * k : 2 * g * (k + 1)] * portions[k]
            summed = summed + pltpu.roll(summed, g, 1)
            intensity = dot(jnp.concatenate(split(summed), axis=1), up_cols[...])
            resist = 1.0 / (1.0 + jnp.exp(-SHARPNESS * (intensity - THRESHOLD)))
            goal = target_ref[0, r : r + edge, :].astype(jnp.float32)
            value = (2.0 * SHARPNESS) * (resist - goal) * resist * (1.0 - resist)
            slope[r : r + edge, :] = value.astype(BF16)

    def adjoint(field):
        low = dot(up_cols[: 2 * g, :], slope[...])
        low = low[:g] + low[g:]
        low = dot(jnp.concatenate(split(low), axis=0), down_cols[...])
        low = (low[:g, : 2 * g] + low[:g, 2 * g :]) + low[g:, : 2 * g]
        weighted = field * jnp.concatenate([jnp.concatenate([low] * quarters, axis=1)] * 2, axis=0)
        high, rest = split(weighted)
        back = dot(row_back[...], high)
        back = (back[: 2 * f] + back[2 * f :]) + dot(row_back[: 2 * f, :], rest)
        tall = jnp.concatenate(
            [
                jnp.concatenate([back[:f, 4 * f * k : 4 * f * (k + 1)], back[f:, 4 * f * k : 4 * f * (k + 1)]], axis=1)
                for k in range(quarters)
            ],
            axis=0,
        )
        m = quarters * f
        turned = dot(jnp.concatenate(split(tall), axis=0), lane_back[...])
        turned = (turned[:m, : 4 * f] + turned[:m, 4 * f :]) + turned[m:, : 4 * f]
        first, second = h_one * turned, h_two * turned
        real = jnp.zeros((f, 4 * f), jnp.float32)
        imag = jnp.zeros((f, 4 * f), jnp.float32)
        for k in range(quarters):
            real = real + first[k * f : (k + 1) * f] * portions[k]
            imag = imag + second[k * f : (k + 1) * f] * portions[k]
        real = real + pltpu.roll(real, 2 * f, 1)
        real = real + pltpu.roll(real, f, 1)
        imag = imag + pltpu.roll(imag, 2 * f, 1)
        imag = imag + pltpu.roll(imag, f, 1)
        return jnp.where(lane < 2 * f, real, imag)

    def tails(packed):
        out = dot(jnp.concatenate(split(packed), axis=1), tail_tab[...])
        return out[:, :n], out[:, n:]

    def corners(name, src, from_h, ring):
        for entry in plan[name, "h"]:
            arrived(entry)
        for v in range(2):
            for h in range(2):
                ring[v, h] = src[bands[v], bands[h]] + from_h[h, bands[v], :]
        for entry in plan[name, "vc"]:
            start(entry)

    up_f, down_f = upper.astype(jnp.float32), lower.astype(jnp.float32)
    left_f, right_f = left.astype(jnp.float32), right.astype(jnp.float32)

    def coverage_part(r):
        at_col = lax.broadcasted_iota(jnp.int32, (1, n), 1)
        cols = jnp.where(at_col < edge, 1.0 - 0.5 * left_f, jnp.where(at_col >= far, 1.0 - 0.5 * right_f, 1.0))
        if r == 0:
            return cols * (1.0 - 0.5 * up_f)
        if r == far:
            return cols * (1.0 - 0.5 * down_f)
        return cols

    def covered(src, from_h, from_v, r):
        rows = slice(r, r + edge)
        own = src[rows, :]
        own = jnp.concatenate(
            [own[:, :edge] + from_h[0, rows, :], own[:, edge:far], own[:, far:] + from_h[1, rows, :]], axis=1
        )
        if r == 0:
            own = own + from_v[0]
        if r == far:
            own = own + from_v[1]
        return own * coverage_part(r)

    field, waves = fields(mask_ref[0].astype(BF16))
    write_slope(waves)
    corners("s", shared, from_h_s, ring_s)
    for entry in plan["m", "h"] + plan["m", "v"] + plan["m", "hm"]:
        start(entry)
    packed = adjoint(field)
    adj[...] = packed
    tail_own = tails(packed)
    own_stack = stacked(jnp.concatenate(tail_own, axis=0))
    for entry in plan["s", "hm"] + plan["s", "v"] + plan["s", "vc"]:
        arrived(entry)
    for entry in plan["adj"]:
        start(entry)
    for r in range(0, n, edge):
        rows = slice(r, r + edge)
        gradient = dot(grad_rows[rows, :], own_stack)
        share = shared[rows, :]
        common = covered(shared, from_h_s, from_v_s, r)
        agreed[rows, :] = common
        dual = share - common
        dual_out[0, rows, :] = dual
        mask = mask_ref[0, rows, :]
        mask_out[0, rows, :] = mask - STEP_SIZE * (gradient + PENALTY * (mask - common + dual))

    field, waves = fields(mask_out[0].astype(BF16))
    corners("m", src_mask, from_h_m, ring_m)
    write_slope(waves)
    packed = adjoint(field)
    last_stack = stacked(jnp.concatenate(tails(packed), axis=0))

    for entry in plan["adj"]:
        arrived(entry)

    def joined(tail, tail_left, tail_right):
        return jnp.concatenate(
            [
                jnp.concatenate(
                    [a[:, :edge] + b[:, far:], a[:, edge:far], a[:, far:] + c[:, :edge]], axis=1
                )
                for a, b, c in zip(tail, tail_left, tail_right)
            ],
            axis=0,
        )

    around = [tails(adj_in[to]) for to in range(8)]
    sum_own = stacked(joined(tail_own, around[0], around[1]))
    sum_up = stacked(joined(around[2], around[4], around[5]))
    sum_down = stacked(joined(around[3], around[6], around[7]))
    for entry in plan["m", "hm"] + plan["m", "v"] + plan["m", "vc"]:
        arrived(entry)
    for r in range(0, n, edge):
        rows = slice(r, r + edge)
        summed = dot(grad_rows[rows, :], sum_own)
        if r == 0:
            summed = summed + dot(grad_rows[far:, :], sum_up)
        if r == far:
            summed = summed + dot(grad_rows[:edge, :], sum_down)
        before = agreed[rows, :]
        mean_mask = covered(src_mask, from_h_m, from_v_m, r)
        common = mean_mask - STEP_SIZE * (summed * coverage_part(r) + PENALTY * (mean_mask - before))
        mask = mask_out[0, rows, :]
        dual = dual_out[0, rows, :] + mask - common
        dual_out[0, rows, :] = dual
        gradient = dot(grad_rows[rows, :], last_stack)
        mask_out[0, rows, :] = mask - STEP_SIZE * (gradient + PENALTY * (mask - common + dual))

    for name in ("s", "m"):
        for part in ("h", "hm", "v", "vc"):
            for entry in plan[name, part]:
                sent(entry)
    for entry in plan["adj"]:
        sent(entry)


def per_device(count, mask_init, dual_init, target, kernels, weights):
    n = mask_init.shape[-1]
    edge = INTERSECTION
    f = int(round(kernels.shape[-1] ** 0.5))
    quarters = kernels.shape[0] // 2
    tables = [jnp.asarray(t) for t in host_tables(n, f)]
    arranged = kernels.reshape(quarters, 2, 2, f, f).transpose(0, 3, 1, 2, 4).reshape(quarters * f, 4 * f)
    f32 = jnp.float32
    whole = pl.BlockSpec(memory_space=pltpu.VMEM)
    return pl.pallas_call(
        functools.partial(body, n, f, edge, count),
        out_shape=(jax.ShapeDtypeStruct((1, n, n), f32), jax.ShapeDtypeStruct((1, n, n), f32)),
        in_specs=[whole] * 4 + [pl.BlockSpec(memory_space=pltpu.SMEM)] + [whole] * len(tables),
        out_specs=(whole, whole),
        scratch_shapes=[
            pltpu.VMEM((n, n), f32),
            pltpu.VMEM((2, 2, edge, edge), f32),
            pltpu.VMEM((2, 2, edge, edge), f32),
            pltpu.VMEM((2, n, edge), f32),
            pltpu.VMEM((2, n, edge), f32),
            pltpu.VMEM((2, edge, n), f32),
            pltpu.VMEM((2, edge, n), f32),
            pltpu.VMEM((n, n), f32),
            pltpu.VMEM((n, n), BF16),
            pltpu.VMEM((f, 4 * f), f32),
            pltpu.VMEM((8, f, 4 * f), f32),
            pltpu.SemaphoreType.DMA((40,)),
            pltpu.SemaphoreType.DMA((40,)),
        ],
        compiler_params=pltpu.CompilerParams(
            collective_id=0, has_side_effects=True, vmem_limit_bytes=48 * 1024 * 1024
        ),
    )(mask_init, dual_init, target, arranged, weights, *tables)


def solution(mesh):
    tile = P(("region", "ty"), None, None)
    return jax.shard_map(
        functools.partial(per_device, mesh.shape["ty"]),
        mesh=mesh,
        in_specs=(tile, tile, tile, P(), P()),
        out_specs=(tile, tile),
        check_vma=False,
    )
```

```python
import functools

import jax
import jax.numpy as jnp
import numpy as np
from jax import lax
from jax.experimental import pallas as pl
from jax.experimental.pallas import tpu as pltpu
from jax.sharding import PartitionSpec as P

GRID_COLS = 4
INTERSECTION = 128
SHARPNESS = 8.0
THRESHOLD = 0.3
STEP_SIZE = 0.25
PENALTY = 1.0
MESH = pl.DeviceIdType.MESH
BF16 = jnp.bfloat16


def split_host(table):
    table = table.astype(np.float32)
    high = table.astype(BF16)
    low = (table - high.astype(np.float32)).astype(BF16)
    return high, low


def host_tables(n, f):
    g = 2 * f
    freq = np.arange(f) - f // 2
    phase = 2.0 * np.pi * ((freq[:, None] * np.arange(n)[None, :]) % n) / n
    cos, sin = np.cos(phase), -np.sin(phase)
    rows = np.concatenate([cos, sin], 0)
    rows_hi, rows_lo = split_host(rows)
    row_side = np.concatenate([rows_hi, rows_lo], 0)
    col_wide = np.concatenate([np.tile(cos.T, (1, 4)), np.tile(sin.T, (1, 4))], 1)
    col_side = split_host(col_wide)[0]
    coarse = 2.0 * np.pi * ((np.arange(g)[:, None] * freq[None, :]) % g) / g
    er, ei = np.cos(coarse), np.sin(coarse)
    pair = np.eye(2)
    to_real = np.kron(pair, np.concatenate([er.T, -ei.T], 0))
    to_imag = np.kron(pair, np.concatenate([ei.T, er.T], 0))
    lane_turn = np.concatenate([to_real, to_imag], 1)
    lane_fwd = np.concatenate(split_host(lane_turn / (n * n)), 1)
    lane_back = np.concatenate(split_host(lane_turn.T), 1)
    row_turn = np.concatenate([np.concatenate([er, -ei], 1), np.concatenate([ei, er], 1)], 0)
    turn_hi, turn_lo = split_host(row_turn)
    row_fwd = np.concatenate([turn_hi, turn_lo, turn_hi, turn_lo], 1)
    row_back = np.concatenate(split_host(row_turn.T), 0)
    half = np.arange(-(f - 1), f)
    angle = np.arange(n)[:, None] * f * 2 - np.arange(g)[None, :] * n
    spread = np.cos(2.0 * np.pi * ((angle[..., None] * half) % (n * g)) / (n * g)).sum(-1) / g
    s_hi, s_lo = split_host(spread)
    up_cols = np.concatenate([s_hi.T, s_lo.T, s_hi.T, s_lo.T], 0)
    er_low, ei_low = rows_hi[:f].T, -rows_hi[f:].T
    low_turn = np.concatenate([np.concatenate([er_low, -ei_low], 1), np.concatenate([ei_low, er_low], 1)], 0)
    up_rows = np.concatenate([low_turn, low_turn], 1)
    down_cols = np.concatenate([s_hi, s_hi, s_lo, s_lo], 1)
    scale = 2.0 / (n * n)
    c_hi, c_lo = split_host(cos * scale)
    t_hi, t_lo = split_host(sin * scale)
    tail_r = np.concatenate([c_hi, c_lo, t_hi, t_lo], 0)
    tail_i = np.concatenate([-t_hi, -t_lo, c_hi, c_lo], 0)
    tail = np.concatenate([tail_r, tail_i], 1)
    tail_tab = np.concatenate([tail, tail], 0)
    grad_rows = np.concatenate([rows_hi.T, rows_lo.T, rows_hi.T, rows_lo.T], 1)
    return [
        np.asarray(t, dtype=BF16)
        for t in (row_side, col_side, lane_fwd, row_fwd, up_cols, up_rows, down_cols, row_back, lane_back, tail_tab, grad_rows)
    ]


def dot(a, b):
    return lax.dot_general(a, b, (((1,), (0,)), ((), ())), preferred_element_type=jnp.float32)


def split(x):
    high = x.astype(BF16)
    return high, (x - high.astype(jnp.float32)).astype(BF16)


def stacked(x):
    high, low = split(x)
    return jnp.concatenate([high, high, low, low], axis=0)


def body(
    n, f, edge, count,
    *refs,
):
    ins, refs = refs[:16], refs[16:]
    mask_out, dual_out, common_out = refs[:3]
    held, refs = refs[3:19], refs[19:]
    mask_ref, dual_ref, target_ref, k_ref, w_ref = held[:5]
    row_side, col_side, lane_fwd, row_fwd, up_cols, up_rows, down_cols, row_back, lane_back, tail_tab, grad_rows = held[5:]
    (
        h_sc, load_sem, shared, ring_s, ring_m, from_h_s, from_h_m, from_v_s, from_v_m, agreed, slope, adj, adj_in,
        send_sem, recv_sem,
    ) = refs
    loads = [pltpu.make_async_copy(src, dst, load_sem.at[i]) for i, (src, dst) in enumerate(zip(ins, held))]
    for i in (0, 1, 3, 4, 5, 6, 7, 8, 9, 10, 2, 11, 12, 13, 14, 15):
        loads[i].start()
    far = n - edge
    g = 2 * f
    me = lax.axis_index("ty")
    row, col = me // GRID_COLS, me % GRID_COLS
    grid_rows = count // GRID_COLS
    left, right = col > 0, col < GRID_COLS - 1
    upper, lower = row > 0, row < grid_rows - 1
    near = [
        (-1, left), (1, right), (-GRID_COLS, upper), (GRID_COLS, lower),
        (-GRID_COLS - 1, jnp.logical_and(upper, left)), (-GRID_COLS + 1, jnp.logical_and(upper, right)),
        (GRID_COLS - 1, jnp.logical_and(lower, left)), (GRID_COLS + 1, jnp.logical_and(lower, right)),
    ]
    opposite = [1, 0, 3, 2, 7, 6, 5, 4]

    barrier = pltpu.get_barrier_semaphore()
    for shift, there in near:
        @pl.when(there)
        def _(shift=shift):
            pl.semaphore_signal(barrier, inc=1, device_id={"ty": me + shift}, device_id_type=MESH)

    counter = [0]

    def remote(src, dst, to):
        index = counter[0]
        counter[0] += 1
        copy = pltpu.make_async_remote_copy(
            src_ref=src, dst_ref=dst, send_sem=send_sem.at[index], recv_sem=recv_sem.at[index],
            device_id={"ty": me + near[to][0]}, device_id_type=MESH,
        )
        return copy, near[to][1], near[opposite[to]][1]

    def start(entry):
        pl.when(entry[1])(entry[0].start)

    def arrived(entry):
        pl.when(entry[2])(entry[0].wait_recv)

    def sent(entry):
        pl.when(entry[1])(entry[0].wait_send)

    bands = (pl.ds(0, edge), pl.ds(far, edge))
    middle = pl.ds(edge, far - edge)

    def side_copies(src, dst, rows):
        return [
            remote(src.at[rows, bands[0]], dst.at[1, rows, :], 0),
            remote(src.at[rows, bands[1]], dst.at[0, rows, :], 1),
        ]

    src_mask = mask_ref.at[0]
    plan = {}
    for name, src, from_h, from_v, ring in (
        ("s", shared, from_h_s, from_v_s, ring_s),
        ("m", src_mask, from_h_m, from_v_m, ring_m),
    ):
        plan[name, "h"] = side_copies(src, from_h, bands[0]) + side_copies(src, from_h, bands[1])
        plan[name, "hm"] = side_copies(src, from_h, middle)
        plan[name, "v"] = [
            remote(src.at[bands[0], middle], from_v.at[1, :, middle], 2),
            remote(src.at[bands[1], middle], from_v.at[0, :, middle], 3),
        ]
        plan[name, "vc"] = [
            remote(ring.at[v, h], from_v.at[1 - v, :, bands[h]], 2 + v) for v in range(2) for h in range(2)
        ]
    plan["adj"] = [remote(adj, adj_in.at[opposite[to]], to) for to in range(8)]

    for h in range(2):
        @pl.when(jnp.logical_not(near[h][1]))
        def _(h=h):
            from_h_s[h] = jnp.zeros((n, edge), jnp.float32)
            from_h_m[h] = jnp.zeros((n, edge), jnp.float32)

        @pl.when(jnp.logical_not(near[2 + h][1]))
        def _(h=h):
            from_v_s[h] = jnp.zeros((edge, n), jnp.float32)
            from_v_m[h] = jnp.zeros((edge, n), jnp.float32)
    for to in range(8):
        @pl.when(jnp.logical_not(near[to][1]))
        def _(to=to):
            adj_in[to] = jnp.zeros((f, 4 * f), jnp.float32)

    loads[0].wait()
    loads[1].wait()
    shared[...] = mask_ref[0] + dual_ref[0]
    expected = sum(there.astype(jnp.int32) for _, there in near)
    pl.semaphore_wait(barrier, expected)

    for entry in plan["s", "h"] + plan["s", "v"] + plan["s", "hm"]:
        start(entry)

    loads[3].wait()
    loads[4].wait()
    quarters = w_ref.shape[0] // 2
    lane = lax.broadcasted_iota(jnp.int32, (1, 4 * f), 1)
    total = w_ref[0]
    for k in range(1, w_ref.shape[0]):
        total = total + w_ref[k]
    portions = [
        jnp.where(lane < 2 * f, w_ref[2 * k], w_ref[2 * k + 1]) / jnp.full((1, 4 * f), total, jnp.float32)
        for k in range(quarters)
    ]
    for k in range(quarters):
        rows_of = []
        for j in range(4):
            flat = k_ref.at[2 * k + j // 2]
            rows_of.append(
                jnp.concatenate([flat[j % 2 : j % 2 + 1, 4 * f * a : 4 * f * (a + 1)] for a in range(f // 4)], axis=0)
            )
        for b in range(4):
            value = rows_of[b]
            for j in range(4):
                if j != b:
                    value = jnp.where(lane // f == j, pltpu.roll(rows_of[j], (j - b) % 4 * f, 1), value)
            h_sc[pl.ds(k * f + b, f // 4, stride=4), :] = value
    h_one = h_sc[...]
    is_real = (lane // f) % 2 == 0
    h_two = jnp.where(is_real, -pltpu.roll(h_one, 3 * f, 1), pltpu.roll(h_one, f, 1))

    waited = set()

    def need(*which):
        for i in which:
            if i not in waited:
                waited.add(i)
                loads[i].wait()

    def fields(mask_low):
        need(5, 6, 7, 8)
        part = dot(row_side[...], mask_low)
        part = part[: 2 * f] + part[2 * f :]
        grid = dot(jnp.concatenate(split(part), axis=0), col_side[...])
        w = 8 * f
        grid = grid[: 2 * f] + grid[2 * f :]
        real = grid[:f, : 4 * f] - grid[f:, 4 * f :]
        imag = grid[:f, 4 * f :] + grid[f:, : 4 * f]
        real = jnp.concatenate([real] * quarters, axis=0)
        imag = jnp.concatenate([imag] * quarters, axis=0)
        gated = h_one * real + h_two * imag
        turned = dot(jnp.concatenate(split(gated), axis=0), lane_fwd[...])
        m = quarters * f
        turned = (turned[:m, :w] + turned[:m, w:]) + turned[m:, :w]
        wide = jnp.concatenate(
            [
                jnp.concatenate([turned[k * f : (k + 1) * f, : 4 * f], turned[k * f : (k + 1) * f, 4 * f :]], axis=0)
                for k in range(quarters)
            ],
            axis=1,
        )
        return dot(row_fwd[...], stacked(wide)), jnp.concatenate(split(wide), axis=0)

    def write_slope(waves):
        need(9, 10, 2)
        for r in range(0, n, edge):
            real = dot(up_rows[r : r + edge, :], waves)
            imag = dot(up_rows[n + r : n + r + edge, :], waves)
            energy = real * real + imag * imag
            summed = energy[:, : 2 * g] * portions[0]
            for k in range(1, quarters):
                summed = summed + energy[:, 2 * g * k : 2 * g * (k + 1)] * portions[k]
            summed = summed + pltpu.roll(summed, g, 1)
            intensity = dot(jnp.concatenate(split(summed), axis=1), up_cols[...])
            resist = 1.0 / (1.0 + jnp.exp(-SHARPNESS * (intensity - THRESHOLD)))
            goal = target_ref[0, r : r + edge, :].astype(jnp.float32)
            value = (2.0 * SHARPNESS) * (resist - goal) * resist * (1.0 - resist)
            slope[r : r + edge, :] = value.astype(BF16)

    def adjoint(field):
        need(11, 12, 13)
        low = dot(up_cols[: 2 * g, :], slope[...])
        low = low[:g] + low[g:]
        low = dot(jnp.concatenate(split(low), axis=0), down_cols[...])
        low = (low[:g, : 2 * g] + low[:g, 2 * g :]) + low[g:, : 2 * g]
        weighted = field * jnp.concatenate([jnp.concatenate([low] * quarters, axis=1)] * 2, axis=0)
        high, rest = split(weighted)
        back = dot(row_back[...], high)
        back = (back[: 2 * f] + back[2 * f :]) + dot(row_back[: 2 * f, :], rest)
        tall = jnp.concatenate(
            [
                jnp.concatenate([back[:f, 4 * f * k : 4 * f * (k + 1)], back[f:, 4 * f * k : 4 * f * (k + 1)]], axis=1)
                for k in range(quarters)
            ],
            axis=0,
        )
        m = quarters * f
        turned = dot(jnp.concatenate(split(tall), axis=0), lane_back[...])
        turned = (turned[:m, : 4 * f] + turned[:m, 4 * f :]) + turned[m:, : 4 * f]
        first, second = h_one * turned, h_two * turned
        real = jnp.zeros((f, 4 * f), jnp.float32)
        imag = jnp.zeros((f, 4 * f), jnp.float32)
        for k in range(quarters):
            real = real + first[k * f : (k + 1) * f] * portions[k]
            imag = imag + second[k * f : (k + 1) * f] * portions[k]
        real = real + pltpu.roll(real, 2 * f, 1)
        real = real + pltpu.roll(real, f, 1)
        imag = imag + pltpu.roll(imag, 2 * f, 1)
        imag = imag + pltpu.roll(imag, f, 1)
        return jnp.where(lane < 2 * f, real, imag)

    def tails(packed):
        need(14, 15)
        out = dot(jnp.concatenate(split(packed), axis=1), tail_tab[...])
        return out[:, :n], out[:, n:]

    def corners(name, src, from_h, ring):
        for entry in plan[name, "h"]:
            arrived(entry)
        for v in range(2):
            for h in range(2):
                ring[v, h] = src[bands[v], bands[h]] + from_h[h, bands[v], :]
        for entry in plan[name, "vc"]:
            start(entry)

    up_f, down_f = upper.astype(jnp.float32), lower.astype(jnp.float32)
    left_f, right_f = left.astype(jnp.float32), right.astype(jnp.float32)

    def coverage_part(r):
        at_col = lax.broadcasted_iota(jnp.int32, (1, n), 1)
        cols = jnp.where(at_col < edge, 1.0 - 0.5 * left_f, jnp.where(at_col >= far, 1.0 - 0.5 * right_f, 1.0))
        if r == 0:
            return cols * (1.0 - 0.5 * up_f)
        if r == far:
            return cols * (1.0 - 0.5 * down_f)
        return cols

    def covered(src, from_h, from_v, r):
        rows = slice(r, r + edge)
        own = src[rows, :]
        own = jnp.concatenate(
            [own[:, :edge] + from_h[0, rows, :], own[:, edge:far], own[:, far:] + from_h[1, rows, :]], axis=1
        )
        if r == 0:
            own = own + from_v[0]
        if r == far:
            own = own + from_v[1]
        return own * coverage_part(r)

    field, waves = fields(mask_ref[0].astype(BF16))
    write_slope(waves)
    corners("s", shared, from_h_s, ring_s)
    for entry in plan["m", "h"] + plan["m", "v"] + plan["m", "hm"]:
        start(entry)
    packed = adjoint(field)
    adj[...] = packed
    tail_own = tails(packed)
    own_stack = stacked(jnp.concatenate(tail_own, axis=0))
    for entry in plan["s", "hm"] + plan["s", "v"] + plan["s", "vc"]:
        arrived(entry)
    for entry in plan["adj"]:
        start(entry)
    for r in range(0, n, edge):
        rows = slice(r, r + edge)
        gradient = dot(grad_rows[rows, :], own_stack)
        share = shared[rows, :]
        common = covered(shared, from_h_s, from_v_s, r)
        agreed[rows, :] = common
        dual = share - common
        dual_out[0, rows, :] = dual
        mask = mask_ref[0, rows, :]
        mask_out[0, rows, :] = mask - STEP_SIZE * (gradient + PENALTY * (mask - common + dual))

    field, waves = fields(mask_out[0].astype(BF16))
    corners("m", src_mask, from_h_m, ring_m)
    write_slope(waves)
    packed = adjoint(field)
    last_stack = stacked(jnp.concatenate(tails(packed), axis=0))

    for entry in plan["adj"]:
        arrived(entry)

    def joined(tail, tail_left, tail_right):
        return jnp.concatenate(
            [
                jnp.concatenate(
                    [a[:, :edge] + b[:, far:], a[:, edge:far], a[:, far:] + c[:, :edge]], axis=1
                )
                for a, b, c in zip(tail, tail_left, tail_right)
            ],
            axis=0,
        )

    around = [tails(adj_in[to]) for to in range(8)]
    sum_own = stacked(joined(tail_own, around[0], around[1]))
    sum_up = stacked(joined(around[2], around[4], around[5]))
    sum_down = stacked(joined(around[3], around[6], around[7]))
    for entry in plan["m", "hm"] + plan["m", "v"] + plan["m", "vc"]:
        arrived(entry)
    for r in range(0, n, edge):
        rows = slice(r, r + edge)
        summed = dot(grad_rows[rows, :], sum_own)
        if r == 0:
            summed = summed + dot(grad_rows[far:, :], sum_up)
        if r == far:
            summed = summed + dot(grad_rows[:edge, :], sum_down)
        before = agreed[rows, :]
        mean_mask = covered(src_mask, from_h_m, from_v_m, r)
        common = mean_mask - STEP_SIZE * (summed * coverage_part(r) + PENALTY * (mean_mask - before))
        mask = mask_out[0, rows, :]
        dual_out[0, rows, :] = dual_out[0, rows, :] + mask
        common_out[0, rows, :] = common
        gradient = dot(grad_rows[rows, :], last_stack)
        mask_out[0, rows, :] = mask - STEP_SIZE * (gradient + PENALTY * (mask - common))

    for name in ("s", "m"):
        for part in ("h", "hm", "v", "vc"):
            for entry in plan[name, part]:
                sent(entry)
    for entry in plan["adj"]:
        sent(entry)


def per_device(count, mask_init, dual_init, target, kernels, weights):
    n = mask_init.shape[-1]
    edge = INTERSECTION
    f = int(round(kernels.shape[-1] ** 0.5))
    tables = [jnp.asarray(t) for t in host_tables(n, f)]
    f32 = jnp.float32
    whole = pl.BlockSpec(memory_space=pltpu.VMEM)
    far_memory = pl.BlockSpec(memory_space=pltpu.HBM)
    arrays = (mask_init, dual_init, target, kernels, weights, *tables)
    tile = jax.ShapeDtypeStruct((1, n, n), f32)
    ahead, total, common = pl.pallas_call(
        functools.partial(body, n, f, edge, count),
        out_shape=(tile, tile, tile),
        in_specs=[far_memory] * len(arrays),
        out_specs=(whole, whole, whole),
        scratch_shapes=[
            pltpu.SMEM(a.shape, a.dtype) if i == 4 else pltpu.VMEM(a.shape, a.dtype) for i, a in enumerate(arrays)
        ]
        + [
            pltpu.VMEM((kernels.shape[0] // 2 * f, 4 * f), f32),
            pltpu.SemaphoreType.DMA((len(arrays),)),
            pltpu.VMEM((n, n), f32),
            pltpu.VMEM((2, 2, edge, edge), f32),
            pltpu.VMEM((2, 2, edge, edge), f32),
            pltpu.VMEM((2, n, edge), f32),
            pltpu.VMEM((2, n, edge), f32),
            pltpu.VMEM((2, edge, n), f32),
            pltpu.VMEM((2, edge, n), f32),
            pltpu.VMEM((n, n), f32),
            pltpu.VMEM((n, n), BF16),
            pltpu.VMEM((f, 4 * f), f32),
            pltpu.VMEM((8, f, 4 * f), f32),
            pltpu.SemaphoreType.DMA((40,)),
            pltpu.SemaphoreType.DMA((40,)),
        ],
        compiler_params=pltpu.CompilerParams(
            collective_id=0, has_side_effects=True, vmem_limit_bytes=67043328
        ),
    )(*arrays)
    dual = total - common
    return ahead - (STEP_SIZE * PENALTY) * dual, dual


def solution(mesh):
    tile = P(("region", "ty"), None, None)
    return jax.shard_map(
        functools.partial(per_device, mesh.shape["ty"]),
        mesh=mesh,
        in_specs=(tile, tile, tile, P(), P()),
        out_specs=(tile, tile),
        check_vma=False,
    )
```

```python
import functools

import jax
import jax.numpy as jnp
import numpy as np
from jax import lax
from jax.experimental import pallas as pl
from jax.experimental.pallas import tpu as pltpu
from jax.sharding import PartitionSpec as P

GRID_COLS = 4
INTERSECTION = 128
SHARPNESS = 8.0
THRESHOLD = 0.3
STEP_SIZE = 0.25
PENALTY = 1.0
MESH = pl.DeviceIdType.MESH
BF16 = jnp.bfloat16


def split_host(table):
    table = table.astype(np.float32)
    high = table.astype(BF16)
    low = (table - high.astype(np.float32)).astype(BF16)
    return high, low


def host_tables(n, f):
    g = 2 * f
    freq = np.arange(f) - f // 2
    phase = 2.0 * np.pi * ((freq[:, None] * np.arange(n)[None, :]) % n) / n
    cos, sin = np.cos(phase), -np.sin(phase)
    rows = np.concatenate([cos, sin], 0)
    rows_hi, rows_lo = split_host(rows)
    row_side = np.concatenate([rows_hi, rows_lo], 0)
    col_wide = np.concatenate([np.tile(cos.T, (1, 4)), np.tile(sin.T, (1, 4))], 1)
    col_side = split_host(col_wide)[0]
    coarse = 2.0 * np.pi * ((np.arange(g)[:, None] * freq[None, :]) % g) / g
    er, ei = np.cos(coarse), np.sin(coarse)
    pair = np.eye(2)
    to_real = np.kron(pair, np.concatenate([er.T, -ei.T], 0))
    to_imag = np.kron(pair, np.concatenate([ei.T, er.T], 0))
    lane_turn = np.concatenate([to_real, to_imag], 1)
    lane_fwd = np.concatenate(split_host(lane_turn / (n * n)), 1)
    lane_back = np.concatenate(split_host(lane_turn.T), 1)
    row_turn = np.concatenate([np.concatenate([er, -ei], 1), np.concatenate([ei, er], 1)], 0)
    turn_hi, turn_lo = split_host(row_turn)
    row_fwd = np.concatenate([turn_hi, turn_lo, turn_hi, turn_lo], 1)
    row_back = np.concatenate(split_host(row_turn.T), 0)
    half = np.arange(-(f - 1), f)
    angle = np.arange(n)[:, None] * f * 2 - np.arange(g)[None, :] * n
    spread = np.cos(2.0 * np.pi * ((angle[..., None] * half) % (n * g)) / (n * g)).sum(-1) / g
    s_hi, s_lo = split_host(spread)
    up_cols = np.concatenate([s_hi.T, s_lo.T, s_hi.T, s_lo.T], 0)
    er_low, ei_low = rows_hi[:f].T, -rows_hi[f:].T
    low_turn = np.concatenate([np.concatenate([er_low, -ei_low], 1), np.concatenate([ei_low, er_low], 1)], 0)
    up_rows = np.concatenate([low_turn, low_turn], 1)
    down_cols = np.concatenate([s_hi, s_hi, s_lo, s_lo], 1)
    scale = 2.0 / (n * n)
    c_hi, c_lo = split_host(cos * scale)
    t_hi, t_lo = split_host(sin * scale)
    tail_r = np.concatenate([c_hi, c_lo, t_hi, t_lo], 0)
    tail_i = np.concatenate([-t_hi, -t_lo, c_hi, c_lo], 0)
    tail = np.concatenate([tail_r, tail_i], 1)
    tail_tab = np.concatenate([tail, tail], 0)
    grad_rows = np.concatenate([rows_hi.T, rows_lo.T, rows_hi.T, rows_lo.T], 1)
    return [
        np.asarray(t, dtype=BF16)
        for t in (row_side, col_side, lane_fwd, row_fwd, up_cols, up_rows, down_cols, row_back, lane_back, tail_tab, grad_rows)
    ]


def dot(a, b):
    return lax.dot_general(a, b, (((1,), (0,)), ((), ())), preferred_element_type=jnp.float32)


def split(x):
    high = x.astype(BF16)
    return high, (x - high.astype(jnp.float32)).astype(BF16)


def stacked(x):
    high, low = split(x)
    return jnp.concatenate([high, high, low, low], axis=0)


def body(
    n, f, edge, count,
    *refs,
):
    ins, refs = refs[:16], refs[16:]
    mask_out, dual_out = refs[:2]
    held, refs = refs[2:18], refs[18:]
    mask_ref, dual_ref, target_ref, k_ref, w_ref = held[:5]
    row_side, col_side, lane_fwd, row_fwd, up_cols, up_rows, down_cols, row_back, lane_back, tail_tab, grad_rows = held[5:]
    (
        h_sc, load_sem, shared, ring_s, ring_m, from_h_s, from_h_m, from_v_s, from_v_m, agreed, slope, adj, adj_in,
        send_sem, recv_sem,
    ) = refs
    loads = [pltpu.make_async_copy(src, dst, load_sem.at[i]) for i, (src, dst) in enumerate(zip(ins, held))]
    for i in (0, 1, 3, 4, 5, 6, 7, 8, 9, 10, 2, 11, 12, 13, 14, 15):
        loads[i].start()
    far = n - edge
    g = 2 * f
    me = lax.axis_index("ty")
    row, col = me // GRID_COLS, me % GRID_COLS
    grid_rows = count // GRID_COLS
    left, right = col > 0, col < GRID_COLS - 1
    upper, lower = row > 0, row < grid_rows - 1
    near = [
        (-1, left), (1, right), (-GRID_COLS, upper), (GRID_COLS, lower),
        (-GRID_COLS - 1, jnp.logical_and(upper, left)), (-GRID_COLS + 1, jnp.logical_and(upper, right)),
        (GRID_COLS - 1, jnp.logical_and(lower, left)), (GRID_COLS + 1, jnp.logical_and(lower, right)),
    ]
    opposite = [1, 0, 3, 2, 7, 6, 5, 4]

    barrier = pltpu.get_barrier_semaphore()
    for shift, there in near:
        @pl.when(there)
        def _(shift=shift):
            pl.semaphore_signal(barrier, inc=1, device_id={"ty": me + shift}, device_id_type=MESH)

    counter = [0]

    def remote(src, dst, to):
        index = counter[0]
        counter[0] += 1
        copy = pltpu.make_async_remote_copy(
            src_ref=src, dst_ref=dst, send_sem=send_sem.at[index], recv_sem=recv_sem.at[index],
            device_id={"ty": me + near[to][0]}, device_id_type=MESH,
        )
        return copy, near[to][1], near[opposite[to]][1]

    def start(entry):
        pl.when(entry[1])(entry[0].start)

    def arrived(entry):
        pl.when(entry[2])(entry[0].wait_recv)

    def sent(entry):
        pl.when(entry[1])(entry[0].wait_send)

    bands = (pl.ds(0, edge), pl.ds(far, edge))
    middle = pl.ds(edge, far - edge)

    def side_copies(src, dst, rows):
        return [
            remote(src.at[rows, bands[0]], dst.at[1, rows, :], 0),
            remote(src.at[rows, bands[1]], dst.at[0, rows, :], 1),
        ]

    src_mask = mask_ref.at[0]
    plan = {}
    for name, src, from_h, from_v, ring in (
        ("s", shared, from_h_s, from_v_s, ring_s),
        ("m", src_mask, from_h_m, from_v_m, ring_m),
    ):
        plan[name, "h"] = side_copies(src, from_h, bands[0]) + side_copies(src, from_h, bands[1])
        plan[name, "hm"] = side_copies(src, from_h, middle)
        plan[name, "v"] = [
            remote(src.at[bands[0], middle], from_v.at[1, :, middle], 2),
            remote(src.at[bands[1], middle], from_v.at[0, :, middle], 3),
        ]
        plan[name, "vc"] = [
            remote(ring.at[v, h], from_v.at[1 - v, :, bands[h]], 2 + v) for v in range(2) for h in range(2)
        ]
    plan["adj"] = [remote(adj, adj_in.at[opposite[to]], to) for to in range(8)]

    for h in range(2):
        @pl.when(jnp.logical_not(near[h][1]))
        def _(h=h):
            from_h_s[h] = jnp.zeros((n, edge), jnp.float32)
            from_h_m[h] = jnp.zeros((n, edge), jnp.float32)

        @pl.when(jnp.logical_not(near[2 + h][1]))
        def _(h=h):
            from_v_s[h] = jnp.zeros((edge, n), jnp.float32)
            from_v_m[h] = jnp.zeros((edge, n), jnp.float32)
    for to in range(8):
        @pl.when(jnp.logical_not(near[to][1]))
        def _(to=to):
            adj_in[to] = jnp.zeros((f, 4 * f), jnp.float32)

    loads[0].wait()
    loads[1].wait()
    shared[...] = mask_ref[0] + dual_ref[0]
    expected = sum(there.astype(jnp.int32) for _, there in near)
    pl.semaphore_wait(barrier, expected)

    for entry in plan["s", "h"] + plan["s", "v"] + plan["s", "hm"]:
        start(entry)

    loads[3].wait()
    loads[4].wait()
    quarters = w_ref.shape[0] // 2
    lane = lax.broadcasted_iota(jnp.int32, (1, 4 * f), 1)
    total = w_ref[0]
    for k in range(1, w_ref.shape[0]):
        total = total + w_ref[k]
    portions = [
        jnp.where(lane < 2 * f, w_ref[2 * k], w_ref[2 * k + 1]) / jnp.full((1, 4 * f), total, jnp.float32)
        for k in range(quarters)
    ]
    for k in range(quarters):
        rows_of = []
        for j in range(4):
            flat = k_ref.at[2 * k + j // 2]
            rows_of.append(
                jnp.concatenate([flat[j % 2 : j % 2 + 1, 4 * f * a : 4 * f * (a + 1)] for a in range(f // 4)], axis=0)
            )
        for b in range(4):
            value = rows_of[b]
            for j in range(4):
                if j != b:
                    value = jnp.where(lane // f == j, pltpu.roll(rows_of[j], (j - b) % 4 * f, 1), value)
            h_sc[pl.ds(k * f + b, f // 4, stride=4), :] = value
    h_one = h_sc[...]
    is_real = (lane // f) % 2 == 0
    h_two = jnp.where(is_real, -pltpu.roll(h_one, 3 * f, 1), pltpu.roll(h_one, f, 1))

    waited = set()

    def need(*which):
        for i in which:
            if i not in waited:
                waited.add(i)
                loads[i].wait()

    def fields(mask_low):
        need(5, 6, 7, 8)
        part = dot(row_side[...], mask_low)
        part = part[: 2 * f] + part[2 * f :]
        grid = dot(jnp.concatenate(split(part), axis=0), col_side[...])
        w = 8 * f
        grid = grid[: 2 * f] + grid[2 * f :]
        real = grid[:f, : 4 * f] - grid[f:, 4 * f :]
        imag = grid[:f, 4 * f :] + grid[f:, : 4 * f]
        real = jnp.concatenate([real] * quarters, axis=0)
        imag = jnp.concatenate([imag] * quarters, axis=0)
        gated = h_one * real + h_two * imag
        turned = dot(jnp.concatenate(split(gated), axis=0), lane_fwd[...])
        m = quarters * f
        turned = (turned[:m, :w] + turned[:m, w:]) + turned[m:, :w]
        wide = jnp.concatenate(
            [
                jnp.concatenate([turned[k * f : (k + 1) * f, : 4 * f], turned[k * f : (k + 1) * f, 4 * f :]], axis=0)
                for k in range(quarters)
            ],
            axis=1,
        )
        return dot(row_fwd[...], stacked(wide)), jnp.concatenate(split(wide), axis=0)

    def write_slope(waves):
        need(9, 10, 2)
        for r in range(0, n, edge):
            real = dot(up_rows[r : r + edge, :], waves)
            imag = dot(up_rows[n + r : n + r + edge, :], waves)
            energy = real * real + imag * imag
            summed = energy[:, : 2 * g] * portions[0]
            for k in range(1, quarters):
                summed = summed + energy[:, 2 * g * k : 2 * g * (k + 1)] * portions[k]
            summed = summed + pltpu.roll(summed, g, 1)
            intensity = dot(jnp.concatenate(split(summed), axis=1), up_cols[...])
            resist = 1.0 / (1.0 + jnp.exp(-SHARPNESS * (intensity - THRESHOLD)))
            goal = target_ref[0, r : r + edge, :].astype(jnp.float32)
            value = (2.0 * SHARPNESS) * (resist - goal) * resist * (1.0 - resist)
            slope[r : r + edge, :] = value.astype(BF16)

    def adjoint(field):
        need(11, 12, 13)
        low = dot(up_cols[: 2 * g, :], slope[...])
        low = low[:g] + low[g:]
        low = dot(jnp.concatenate(split(low), axis=0), down_cols[...])
        low = (low[:g, : 2 * g] + low[:g, 2 * g :]) + low[g:, : 2 * g]
        weighted = field * jnp.concatenate([jnp.concatenate([low] * quarters, axis=1)] * 2, axis=0)
        high, rest = split(weighted)
        back = dot(row_back[...], high)
        back = (back[: 2 * f] + back[2 * f :]) + dot(row_back[: 2 * f, :], rest)
        tall = jnp.concatenate(
            [
                jnp.concatenate([back[:f, 4 * f * k : 4 * f * (k + 1)], back[f:, 4 * f * k : 4 * f * (k + 1)]], axis=1)
                for k in range(quarters)
            ],
            axis=0,
        )
        m = quarters * f
        turned = dot(jnp.concatenate(split(tall), axis=0), lane_back[...])
        turned = (turned[:m, : 4 * f] + turned[:m, 4 * f :]) + turned[m:, : 4 * f]
        first, second = h_one * turned, h_two * turned
        real = jnp.zeros((f, 4 * f), jnp.float32)
        imag = jnp.zeros((f, 4 * f), jnp.float32)
        for k in range(quarters):
            real = real + first[k * f : (k + 1) * f] * portions[k]
            imag = imag + second[k * f : (k + 1) * f] * portions[k]
        real = real + pltpu.roll(real, 2 * f, 1)
        real = real + pltpu.roll(real, f, 1)
        imag = imag + pltpu.roll(imag, 2 * f, 1)
        imag = imag + pltpu.roll(imag, f, 1)
        return jnp.where(lane < 2 * f, real, imag)

    def tails(packed):
        need(14, 15)
        out = dot(jnp.concatenate(split(packed), axis=1), tail_tab[...])
        return out[:, :n], out[:, n:]

    def corners(name, src, from_h, ring):
        for entry in plan[name, "h"]:
            arrived(entry)
        for v in range(2):
            for h in range(2):
                ring[v, h] = src[bands[v], bands[h]] + from_h[h, bands[v], :]
        for entry in plan[name, "vc"]:
            start(entry)

    up_f, down_f = upper.astype(jnp.float32), lower.astype(jnp.float32)
    left_f, right_f = left.astype(jnp.float32), right.astype(jnp.float32)

    def coverage_part(r):
        at_col = lax.broadcasted_iota(jnp.int32, (1, n), 1)
        cols = jnp.where(at_col < edge, 1.0 - 0.5 * left_f, jnp.where(at_col >= far, 1.0 - 0.5 * right_f, 1.0))
        if r == 0:
            return cols * (1.0 - 0.5 * up_f)
        if r == far:
            return cols * (1.0 - 0.5 * down_f)
        return cols

    def covered(src, from_h, from_v, r):
        rows = slice(r, r + edge)
        own = src[rows, :]
        own = jnp.concatenate(
            [own[:, :edge] + from_h[0, rows, :], own[:, edge:far], own[:, far:] + from_h[1, rows, :]], axis=1
        )
        if r == 0:
            own = own + from_v[0]
        if r == far:
            own = own + from_v[1]
        return own * coverage_part(r)

    field, waves = fields(mask_ref[0].astype(BF16))
    write_slope(waves)
    corners("s", shared, from_h_s, ring_s)
    for entry in plan["m", "h"] + plan["m", "v"] + plan["m", "hm"]:
        start(entry)
    packed = adjoint(field)
    adj[...] = packed
    tail_own = tails(packed)
    own_stack = stacked(jnp.concatenate(tail_own, axis=0))
    for entry in plan["s", "hm"] + plan["s", "v"] + plan["s", "vc"]:
        arrived(entry)
    for entry in plan["adj"]:
        start(entry)
    for r in range(0, n, edge):
        rows = slice(r, r + edge)
        gradient = dot(grad_rows[rows, :], own_stack)
        share = shared[rows, :]
        common = covered(shared, from_h_s, from_v_s, r)
        agreed[rows, :] = common
        dual = share - common
        dual_out[0, rows, :] = dual
        mask = mask_ref[0, rows, :]
        mask_out[0, rows, :] = mask - STEP_SIZE * (gradient + PENALTY * (mask - common + dual))

    field, waves = fields(mask_out[0].astype(BF16))
    corners("m", src_mask, from_h_m, ring_m)
    write_slope(waves)
    packed = adjoint(field)
    last_stack = stacked(jnp.concatenate(tails(packed), axis=0))

    for entry in plan["adj"]:
        arrived(entry)

    def joined(tail, tail_left, tail_right):
        return jnp.concatenate(
            [
                jnp.concatenate(
                    [a[:, :edge] + b[:, far:], a[:, edge:far], a[:, far:] + c[:, :edge]], axis=1
                )
                for a, b, c in zip(tail, tail_left, tail_right)
            ],
            axis=0,
        )

    around = [tails(adj_in[to]) for to in range(8)]
    sum_own = stacked(joined(tail_own, around[0], around[1]))
    sum_up = stacked(joined(around[2], around[4], around[5]))
    sum_down = stacked(joined(around[3], around[6], around[7]))
    for entry in plan["m", "hm"] + plan["m", "v"] + plan["m", "vc"]:
        arrived(entry)
    for r in range(0, n, edge):
        rows = slice(r, r + edge)
        summed = dot(grad_rows[rows, :], sum_own)
        if r == 0:
            summed = summed + dot(grad_rows[far:, :], sum_up)
        if r == far:
            summed = summed + dot(grad_rows[:edge, :], sum_down)
        before = agreed[rows, :]
        mean_mask = covered(src_mask, from_h_m, from_v_m, r)
        common = mean_mask - STEP_SIZE * (summed * coverage_part(r) + PENALTY * (mean_mask - before))
        mask = mask_out[0, rows, :]
        dual = dual_out[0, rows, :] + mask - common
        dual_out[0, rows, :] = dual
        gradient = dot(grad_rows[rows, :], last_stack)
        mask_out[0, rows, :] = mask - STEP_SIZE * (gradient + PENALTY * (mask - common + dual))

    for name in ("s", "m"):
        for part in ("h", "hm", "v", "vc"):
            for entry in plan[name, part]:
                sent(entry)
    for entry in plan["adj"]:
        sent(entry)


def per_device(count, mask_init, dual_init, target, kernels, weights):
    n = mask_init.shape[-1]
    edge = INTERSECTION
    f = int(round(kernels.shape[-1] ** 0.5))
    tables = [jnp.asarray(t) for t in host_tables(n, f)]
    f32 = jnp.float32
    whole = pl.BlockSpec(memory_space=pltpu.VMEM)
    far_memory = pl.BlockSpec(memory_space=pltpu.HBM)
    arrays = (mask_init, dual_init, target, kernels, weights, *tables)
    tile = jax.ShapeDtypeStruct((1, n, n), f32)
    return pl.pallas_call(
        functools.partial(body, n, f, edge, count),
        out_shape=(tile, tile),
        in_specs=[far_memory] * len(arrays),
        out_specs=(whole, whole),
        scratch_shapes=[
            pltpu.SMEM(a.shape, a.dtype) if i == 4 else pltpu.VMEM(a.shape, a.dtype) for i, a in enumerate(arrays)
        ]
        + [
            pltpu.VMEM((kernels.shape[0] // 2 * f, 4 * f), f32),
            pltpu.SemaphoreType.DMA((len(arrays),)),
            pltpu.VMEM((n, n), f32),
            pltpu.VMEM((2, 2, edge, edge), f32),
            pltpu.VMEM((2, 2, edge, edge), f32),
            pltpu.VMEM((2, n, edge), f32),
            pltpu.VMEM((2, n, edge), f32),
            pltpu.VMEM((2, edge, n), f32),
            pltpu.VMEM((2, edge, n), f32),
            pltpu.VMEM((n, n), f32),
            pltpu.VMEM((n, n), BF16),
            pltpu.VMEM((f, 4 * f), f32),
            pltpu.VMEM((8, f, 4 * f), f32),
            pltpu.SemaphoreType.DMA((40,)),
            pltpu.SemaphoreType.DMA((40,)),
        ],
        compiler_params=pltpu.CompilerParams(
            collective_id=0, has_side_effects=True, vmem_limit_bytes=48 * 1024 * 1024
        ),
    )(*[pltpu.with_memory_space_constraint(a, pltpu.HBM) for a in arrays])


def solution(mesh):
    tile = P(("region", "ty"), None, None)
    return jax.shard_map(
        functools.partial(per_device, mesh.shape["ty"]),
        mesh=mesh,
        in_specs=(tile, tile, tile, P(), P()),
        out_specs=(tile, tile),
        check_vma=False,
    )
```
